32 devices in a mesh: groups: 2 (over x), row: 16 (over z, y, core).
Axes of the slice: x: 2, y: 2, z: 4, core: 2. Of those that a mesh axis runs over, the one named last changes fastest.
Arguments:
- homolog_embedding: bfloat16 [128, 256, 64], P('groups', 'row'), parts along dimension 0, may hold values from -6 to 6
- pair_state_tiles: bfloat16 [512, 256, 128], P(('groups', 'row')), parts along dimension 0, may hold values from -6 to 6
- alignment_mask: int32 [128, 256], P('groups', 'row'), parts along dimension 0, may hold values 0 or 1
- token_real_mask: int32 [512], P('groups'), parts along dimension 0, may hold values 0 or 1
- lineup_standardize_scaling: float32 [64], replicated, may hold values from 0.1 to 1.9
- former_factor_proj: bfloat16 [64, 32], replicated, may hold values from -0.75 to 0.75
- latter_factor_proj: bfloat16 [64, 32], replicated, may hold values from -0.75 to 0.75
- outer_output_weight: bfloat16 [1024, 128], replicated, may hold values from -0.1875 to 0.1875
- pair_norm_gain: float32 [128], replicated, may hold values from 0.1 to 1.9
- pair_logit_weight: float32 [128, 8], replicated
- content_vector_proj: bfloat16 [64, 256], replicated, may hold values from -0.75 to 0.75
- sigmoid_switch_proj: bfloat16 [64, 256], replicated, may hold values from -0.75 to 0.75
- final_result_proj: bfloat16 [256, 64], replicated, may hold values from -0.375 to 0.375
Outputs:
- alignment_updated: bfloat16 [128, 256, 64], P('groups', 'row'), parts along dimension 0
- pair_updated: bfloat16 [512, 256, 128], P(('groups', 'row')), parts along dimension 0
The draws below stay inside these ranges and needn't reach their ends.
There are 2 independent parts, one for each index of `groups`. The reference program is written for one: setup_inputs(seed, part) draws one part's arguments, and reference() takes and returns one part's arrays. A program takes and returns all parts, laid end to end along the dimension named above; an argument that names none is the same for every part. Nothing has to cross between parts.
All inputs are finite; a program needn't handle non-finite values. No bound on the sum of `alignment_mask` on one device may be relied on, other than what follows from the above.
Results may differ from the reference program's by a relative error of at most 0.007.
Values may be sent and summed in bfloat16 or wider, within the bound.
A program may use at most 128 MiB of HBM per device.

```python
import math
import jax
import jax.numpy as jnp
from jax import lax

LINEUP_FEATURES = 64
C_Z = 128
PRODUCT_FEATURES = 32
AVERAGER_GROUPS = 8
GROUP_FEATURES = 32
HOMOLOG_TOTAL = 64
CROP_RESIDUE_NUM = 256


def draw_pair_logit_weight(key, part):
    first, second = jax.random.split(jax.random.fold_in(key, 7))
    scales = jnp.exp(jax.random.uniform(first, (AVERAGER_GROUPS,), jnp.float32, math.log(0.5), math.log(8.0)))
    entries = jax.random.normal(second, (C_Z, AVERAGER_GROUPS), jnp.float32)
    return entries * scales[None, :] / math.sqrt(C_Z)


def set_ends(values, stream_key, low, high):
    dims = values.shape
    spot = [jax.random.randint(jax.random.fold_in(stream_key, axis), (), 0, dims[axis]) for axis in range(len(dims))]
    values = values.at[tuple(spot)].set(low)
    longest = dims.index(max(dims))
    spot[longest] = (spot[longest] + 1) % dims[longest]
    return values.at[tuple(spot)].set(high)


def block_scale(stream_key, shape, shards, least, high):
    loudness = 1.0
    for axis_at, blocks in shards:
        heights = jax.random.uniform(jax.random.fold_in(jax.random.fold_in(stream_key, 6), axis_at), (blocks,), jnp.float32, least / len(shards), high / len(shards))
        loudness = loudness * jnp.repeat(jnp.exp(heights), shape[axis_at] // blocks).reshape((-1,) + (1,) * (len(shape) - 1 - axis_at))
    return loudness


def noise(stream_key, extent, scale, limit, cuts=(), dtype=jnp.bfloat16):
    loudness = block_scale(stream_key, extent, cuts, -0.22, 0.18) if cuts else 1.0
    result = jax.random.normal(stream_key, extent, jnp.float32) * scale * loudness
    return jnp.minimum(jnp.maximum(result, -limit), limit).astype(dtype)


def setup_inputs(seed: int = 0, part: int = 0) -> dict:
    key_list = jax.random.split(jax.random.key(seed), 14)
    part_splits = jax.random.split(jax.random.fold_in(key_list[13], part), 14)
    return {
        "homolog_embedding": noise(part_splits[0], (HOMOLOG_TOTAL, CROP_RESIDUE_NUM, LINEUP_FEATURES), 1.0, 6.0, ((1, 16),)),
        "pair_state_tiles": noise(part_splits[1], (CROP_RESIDUE_NUM, CROP_RESIDUE_NUM, C_Z), 1.0, 6.0, ((0, 16),)),
        "alignment_mask": set_ends((jax.random.randint(part_splits[2], (HOMOLOG_TOTAL, CROP_RESIDUE_NUM), 0, 4) < 3).astype(jnp.int32), jax.random.fold_in(part_splits[2], 1), 0, 1),
        "token_real_mask": set_ends((jax.random.randint(part_splits[3], (CROP_RESIDUE_NUM,), 0, 8) < 7).astype(jnp.int32), jax.random.fold_in(part_splits[3], 1), 0, 1),
        "lineup_standardize_scaling": jnp.clip(1.0 + 0.18 * jax.random.normal(key_list[4], (LINEUP_FEATURES,), jnp.float32), 0.1, 1.9),
        "former_factor_proj": noise(key_list[5], (LINEUP_FEATURES, PRODUCT_FEATURES), LINEUP_FEATURES ** -0.5, 0.75),
        "latter_factor_proj": noise(key_list[6], (LINEUP_FEATURES, PRODUCT_FEATURES), LINEUP_FEATURES ** -0.5, 0.75),
        "outer_output_weight": noise(key_list[7], (PRODUCT_FEATURES * PRODUCT_FEATURES, C_Z), (PRODUCT_FEATURES * PRODUCT_FEATURES) ** -0.5, 0.1875),
        "pair_norm_gain": jnp.clip(1.0 + 0.18 * jax.random.normal(key_list[8], (C_Z,), jnp.float32), 0.1, 1.9),
        "pair_logit_weight": draw_pair_logit_weight(jax.random.fold_in(key_list[13], 71), part),
        "content_vector_proj": noise(key_list[10], (LINEUP_FEATURES, AVERAGER_GROUPS * GROUP_FEATURES), LINEUP_FEATURES ** -0.5, 0.75),
        "sigmoid_switch_proj": noise(key_list[11], (LINEUP_FEATURES, AVERAGER_GROUPS * GROUP_FEATURES), LINEUP_FEATURES ** -0.5, 0.75),
        "final_result_proj": noise(key_list[12], (AVERAGER_GROUPS * GROUP_FEATURES, LINEUP_FEATURES), (AVERAGER_GROUPS * GROUP_FEATURES) ** -0.5, 0.375),
    }


def layer_normalize(inputs, gain):
    inputs = inputs.astype(jnp.float32)
    center = lax.optimization_barrier(jnp.mean(inputs, axis=-1, keepdims=True))
    spread = lax.optimization_barrier(jnp.mean((inputs - center) ** 2, axis=-1, keepdims=True))
    return (inputs - center) * lax.rsqrt(spread + 1e-05) * gain

def reference(homolog_embedding, pair_state_tiles, alignment_mask, token_real_mask, lineup_standardize_scaling, former_factor_proj, latter_factor_proj, outer_output_weight, pair_norm_gain, pair_logit_weight, content_vector_proj, sigmoid_switch_proj, final_result_proj):
    single_float = jnp.float32
    normed_input = layer_normalize(homolog_embedding, lineup_standardize_scaling).astype(jnp.bfloat16)
    normed_f = normed_input.astype(single_float)
    mask_floating = alignment_mask.astype(single_float)
    left_rows = (jnp.einsum('snc,cd->snd', normed_f, former_factor_proj.astype(single_float)) * mask_floating[:, :, None]).astype(jnp.bfloat16)
    right_rows = (jnp.einsum('snc,cd->snd', normed_f, latter_factor_proj.astype(single_float)) * mask_floating[:, :, None]).astype(jnp.bfloat16)
    tokens = CROP_RESIDUE_NUM
    width = math.gcd(tokens, 64)
    nblocks = tokens // width
    weight_cube = outer_output_weight.astype(single_float).reshape(PRODUCT_FEATURES, PRODUCT_FEATURES, C_Z)
    left_blocks = left_rows.reshape(HOMOLOG_TOTAL, nblocks, width, PRODUCT_FEATURES).transpose(1, 0, 2, 3)
    mask_blocks = mask_floating.reshape(HOMOLOG_TOTAL, nblocks, width).transpose(1, 0, 2)
    right_f = right_rows.astype(single_float)

    def one_block(operands):
        block_left, block_mask = operands
        folded = jnp.einsum('sic,cez->seiz', block_left.astype(single_float), weight_cube).astype(jnp.bfloat16)
        product = jnp.einsum('seiz,sje->ijz', folded.astype(single_float), right_f)
        counts = jnp.einsum('si,sj->ij', block_mask, mask_floating)
        return product / (1.0 + counts)[:, :, None]
    update = lax.map(one_block, (left_blocks, mask_blocks)).reshape(tokens, tokens, C_Z)
    pair_updated = (pair_state_tiles.astype(single_float) + update).astype(jnp.bfloat16)
    pair_normed = layer_normalize(pair_updated, pair_norm_gain)
    logits = jnp.einsum('ijc,ch->hij', pair_normed, pair_logit_weight, precision=lax.Precision.HIGHEST)
    logits = jnp.where(token_real_mask[None, None, :] == 1, logits, -1000000000.0)
    weights = jax.nn.softmax(logits, axis=2).astype(jnp.bfloat16)
    values = jnp.einsum('snc,ck->snk', normed_f, content_vector_proj.astype(single_float)).astype(jnp.bfloat16)
    gate_vals = jax.nn.sigmoid(jnp.einsum('snc,ck->snk', normed_f, sigmoid_switch_proj.astype(single_float)))
    values_heads = values.astype(single_float).reshape(HOMOLOG_TOTAL, tokens, AVERAGER_GROUPS, GROUP_FEATURES)
    average = jnp.einsum('hij,sjhc->sihc', weights.astype(single_float), values_heads).reshape(HOMOLOG_TOTAL, tokens, AVERAGER_GROUPS * GROUP_FEATURES)
    gated_output = (gate_vals * average).astype(jnp.bfloat16)
    update_alignment = jnp.einsum('tpb,bo->tpo', gated_output.astype(single_float), final_result_proj.astype(single_float))
    alignment_updated = (homolog_embedding.astype(single_float) + update_alignment).astype(jnp.bfloat16)
    return (alignment_updated, pair_updated)
```

```python
import functools

import jax
import jax.numpy as jnp
from jax import lax
from jax.experimental import pallas as pl
from jax.experimental.pallas import tpu as pltpu
from jax.sharding import PartitionSpec as P

F32 = jnp.float32
BF = jnp.bfloat16
MESH = pl.DeviceIdType.MESH
NT = (((1,), (1,)), ((), ()))


def mm(a, b):
    return jnp.dot(a, b, preferred_element_type=F32)


def iota(shape, dim):
    return lax.broadcasted_iota(jnp.int32, shape, dim)


def kernel(
    dims,
    x_ref, pair_hbm, mask_ref, tok_ref, scale_ref, former_ref, latter_ref, outw_ref,
    gain_ref, logitw_ref, content_ref, switch_ref, final_ref,
    out_ref, pair_out_hbm,
    gr, gn, fold, n2_sc, lhs_sc, rt_sc, wf_sc, wl_sc, mr_sc, gw_sc, lg_sc, bd_sc, fin_sc,
    gate_sc, a2_sc, pair_in, pair_new,
    r_recv, rz_send, ry_send, rp_send, n_recv, nz_send, ny_send, np_send, in_sem, out_sem,
):
    nz, chunks = dims
    seqs, loc, feat = x_ref.shape
    half = seqs // 2
    lanes = 2 * feat
    pairs = loc // 2
    factor = former_ref.shape[1]
    zdim = outw_ref.shape[1]
    heads = logitw_ref.shape[1]
    width = content_ref.shape[1] // heads
    span = gn.shape[1]
    tiles = factor * seqs // 128
    per = half // chunks
    half_rows = half * loc

    group = lax.axis_index("groups")
    me = lax.axis_index("row")
    core = lax.rem(me, 2)
    yy = lax.rem(me // 2, 2)
    zz = me // 4

    def dev(z, y, c):
        return (z * 2 + y) * 2 + c

    def far(dz):
        return lax.rem(zz + dz, nz)

    partner = dev(zz, yy, 1 - core)
    yside = dev(zz, 1 - yy, core)

    barrier = pltpu.get_barrier_semaphore()
    peers = [dev(far(dz), yy, core) for dz in range(1, nz)] + [yside, partner]
    for peer in peers:
        pl.semaphore_signal(barrier, inc=1, device_id=(group, peer), device_id_type=MESH)

    load = pltpu.make_async_copy(pair_hbm, pair_in, in_sem)
    load.start()

    def rows_of(d):
        return pl.ds(pl.multiple_of(d * loc, loc), loc)

    def r_copy(d, target, sem):
        view = gr.at[:, rows_of(d), :]
        return pltpu.make_async_remote_copy(
            src_ref=view, dst_ref=view, send_sem=sem, recv_sem=r_recv.at[d],
            device_id=(group, target), device_id_type=MESH)

    def n_copy(ch, d, target, sem):
        view = gn.at[pl.ds(ch * per, per), rows_of(d), :]
        return pltpu.make_async_remote_copy(
            src_ref=view, dst_ref=view, send_sem=sem, recv_sem=n_recv.at[ch, d],
            device_id=(group, target), device_id_type=MESH)

    x = x_ref[...].astype(F32)
    center = jnp.mean(x, axis=-1, keepdims=True)
    spread = jnp.mean((x - center) ** 2, axis=-1, keepdims=True)
    normed = ((x - center) * lax.rsqrt(spread + 1e-05) * scale_ref[...][None]).astype(BF).astype(F32)
    n2 = jnp.concatenate(
        [normed[:half].reshape(half_rows, feat), normed[half:].reshape(half_rows, feat)], axis=1)
    n2_sc[...] = n2
    own = rows_of(me)
    gn[:, own, :] = n2.astype(BF).reshape(half, loc, lanes)

    mask = mask_ref[...].astype(F32)
    mask_pad = jnp.concatenate([mask, jnp.zeros((seqs, 128 - loc), F32)], axis=1)
    mask_sq = jnp.concatenate([mask_pad, jnp.zeros((128 - seqs, 128), F32)], axis=0)
    gr[tiles, own, :] = mask_sq.T[:loc].astype(BF)
    proj = jnp.concatenate(
        [former_ref[...].astype(F32), latter_ref[...].astype(F32),
         jnp.zeros((feat, 128 - 2 * factor), F32)], axis=1).astype(BF)

    def rows_for(i):
        packed = n2_sc[pl.ds(i, half, stride=loc), :]
        rows = jnp.concatenate([packed[:, :feat], packed[:, feat:]], axis=0)
        return rows * mask[:, i:i + 1]

    for i2 in range(pairs):
        rows = jnp.concatenate([rows_for(i2), rows_for(i2 + pairs)], axis=0).astype(BF)
        both = mm(rows, proj)
        lhs_sc[i2] = both.astype(BF)
        flipped = both.T
        rt_sc[pl.ds(i2 * factor, factor), :] = flipped[factor:2 * factor]
    low = iota((pairs, 128), 1) < seqs
    for t in range(tiles):
        a = rt_sc[pl.ds(2 * t, pairs, stride=factor), :]
        b = rt_sc[pl.ds(2 * t + 1, pairs, stride=factor), :]
        top = jnp.where(low, a, pltpu.roll(b, seqs, 1))
        bottom = jnp.where(low, pltpu.roll(a, seqs, 1), b)
        gr[t, own, :] = jnp.concatenate([top, bottom], axis=0).astype(BF)

    wf_sc[...] = outw_ref[...].astype(F32)
    for e in range(factor):
        wl_sc[:, e * zdim:(e + 1) * zdim] = wf_sc[pl.ds(e, factor, stride=factor), :].astype(BF)

    pl.semaphore_wait(barrier, nz + 1)
    r_copy(me, yside, ry_send.at[0]).start()
    for dz in range(1, nz):
        r_copy(me, dev(far(dz), yy, core), rz_send.at[dz]).start()
    r_copy(me, partner, rp_send.at[0, 0]).start()
    for ch in range(chunks):
        for dz in range(1, nz):
            n_copy(ch, me, dev(far(dz), yy, core), nz_send.at[ch, dz]).start()

    stride = max(1, pairs // nz)

    def r_relay(dz):
        d = dev(far(dz), yy, core)
        r_copy(d, partner, ry_send.at[dz]).wait_recv()
        r_copy(d, yside, ry_send.at[dz]).start()
        r_copy(d, partner, rp_send.at[0, dz]).start()

    def fold_step(i2, carry):
        left = lhs_sc[i2][:, :factor]
        step = 8
        for e0 in range(0, factor, step):
            res = mm(left, wl_sc[:, e0 * zdim:(e0 + step) * zdim]).astype(BF)
            for e in range(e0, e0 + step):
                part = res[:, (e - e0) * zdim:(e - e0 + 1) * zdim]
                fold[i2, e * seqs:(e + 1) * seqs, :zdim] = part[:seqs]
                fold[i2, e * seqs:(e + 1) * seqs, zdim:] = part[seqs:]
        dz = (i2 + 1) // stride - 1

        @pl.when((lax.rem(i2 + 1, stride) == 0) & (dz >= 1) & (dz < nz))
        def _():
            r_relay(dz)

        return carry

    lax.fori_loop(0, pairs, fold_step, 0)
    for dz in range(max(1, pairs // stride), nz):
        r_relay(dz)
    for ch in range(chunks):
        n_copy(ch, me, yside, ny_send.at[ch, 0]).start()

    for i2 in range(pairs):
        for k in range(2):
            col = mask_sq[:, i2 + k * pairs:i2 + k * pairs + 1]
            mr_sc[i2, :, k * zdim:(k + 1) * zdim] = jnp.broadcast_to(col, (128, zdim)).astype(BF)
    lw = jnp.concatenate([logitw_ref[...], jnp.zeros((zdim, 128 - heads), F32)], axis=1).T[:heads]
    gw = lw * gain_ref[...]
    g0 = gw.astype(BF).astype(F32)
    g1 = (gw - g0).astype(BF).astype(F32)
    g2 = gw - g0 - g1
    flat = jnp.concatenate([g0, g1, g2, jnp.zeros((heads, zdim), F32)], axis=0)
    ones = jnp.concatenate([jnp.zeros((3 * heads, zdim), F32), jnp.ones((heads, zdim), F32)], axis=0)
    gw_sc[...] = jnp.concatenate([flat, flat, ones, ones], axis=1).astype(BF)

    cols = heads * 2 * width
    pick = (iota((heads * width, cols), 0)
            == (iota((heads * width, cols), 1) // (2 * width)) * width
            + iota((heads * width, cols), 1) % width).astype(F32).astype(BF)
    content = mm(content_ref[...], pick)
    wide = cols // 2
    for g in range(2):
        part = jnp.concatenate([content[:, g * wide:(g + 1) * wide]] * heads, axis=0)
        keep = iota(part.shape, 0) // feat == iota(part.shape, 1) // width
        bd_sc[g] = jnp.where(keep, part, 0.0).astype(BF)
    switch = mm(switch_ref[...], pick)
    switch = jnp.concatenate([switch, switch], axis=0)
    keep = iota(switch.shape, 0) // feat == (iota(switch.shape, 1) // width) % 2
    switch = jnp.where(keep, switch, 0.0).astype(BF)
    fin = final_ref[...].astype(F32)
    blocks = []
    for h in range(heads):
        blocks += [fin[h * width:(h + 1) * width]] * 2
    fin = jnp.concatenate(blocks, axis=0)
    fin = jnp.concatenate([fin, fin], axis=1)
    keep = (iota(fin.shape, 0) // width) % 2 == iota(fin.shape, 1) // feat
    fin_sc[...] = jnp.where(keep, fin, 0.0).astype(BF)

    for q in range(4):
        size = half_rows // 4
        pre = mm(n2_sc[q * size:(q + 1) * size, :].astype(BF), switch)
        gate_sc[q * size:(q + 1) * size, :] = jax.nn.sigmoid(pre)

    for dz in range(nz):
        d = dev(far(dz), 1 - yy, core)
        r_copy(d, partner, rp_send.at[1, dz]).wait_recv()
        r_copy(d, partner, rp_send.at[1, dz]).start()
    for ch in range(chunks):
        n_copy(ch, me, partner, np_send.at[ch, 0, 0]).start()
    for y in range(2):
        for dz in range(nz):
            d = dev(far(dz), lax.rem(yy + y, 2), 1 - core)
            r_copy(d, partner, rp_send.at[y, dz]).wait_recv()
    load.wait()

    real = tok_ref[...] == 1
    mean_of = jnp.full((zdim, zdim), 1.0 / zdim, F32).astype(BF)
    rel = pairs // chunks

    def pair_step(i2, carry):
        lhs = jnp.concatenate([gr[t] for t in range(tiles)], axis=1)
        acc = mm(lhs, fold[i2])
        counts = mm(gr[tiles], mr_sc[i2])
        acc = acc / (1.0 + counts)
        for k in range(2):
            i = i2 + k * pairs
            new = (pair_in[i].astype(F32) + acc[:, k * zdim:(k + 1) * zdim]).astype(BF)
            pair_new[i] = new
            cent = new.astype(F32) - mm(new, mean_of)
            hi = cent.astype(BF)
            lo = (cent - hi.astype(F32)).astype(BF)
            sq = cent * cent
            sh = sq.astype(BF)
            sl = (sq - sh.astype(F32)).astype(BF)
            rhs = jnp.concatenate([hi, lo, sh, sl], axis=1)
            res = lax.dot_general(gw_sc[...], rhs, NT, preferred_element_type=F32)
            total = res[:heads] + res[heads:2 * heads] + res[2 * heads:3 * heads]
            logits = total * lax.rsqrt(res[3 * heads:] / zdim + 1e-05)
            logits = jnp.where(real, logits, -1000000000.0)
            for t in range(span // 128):
                lg_sc[t, pl.ds(i, heads, stride=loc), :] = logits[:, t * 128:(t + 1) * 128]
        ch = i2 // rel

        @pl.when(lax.rem(i2, rel) == 0)
        def _():
            for dz in range(1, nz):
                d = dev(far(dz), yy, core)
                n_copy(ch, d, yside, ny_send.at[ch, dz]).wait_recv()
                n_copy(ch, d, yside, ny_send.at[ch, dz]).start()
                n_copy(ch, d, partner, np_send.at[ch, 0, dz]).start()

        @pl.when(lax.rem(i2, rel) == rel - 1)
        def _():
            for dz in range(nz):
                d = dev(far(dz), 1 - yy, core)
                n_copy(ch, d, partner, np_send.at[ch, 1, dz]).wait_recv()
                n_copy(ch, d, partner, np_send.at[ch, 1, dz]).start()

        return carry

    lax.fori_loop(0, pairs, pair_step, 0)
    save = pltpu.make_async_copy(pair_new, pair_out_hbm, out_sem)
    save.start()

    logits = jnp.concatenate([lg_sc[t] for t in range(span // 128)], axis=1)
    top = jnp.max(logits, axis=1, keepdims=True)
    raised = jnp.exp(logits - top)
    weights = (raised / jnp.sum(raised, axis=1, keepdims=True)).astype(BF)

    def average_chunk(ch, carry):
        for y in range(2):
            for dz in range(nz):
                d = dev(far(dz), lax.rem(yy + y, 2), 1 - core)
                n_copy(ch, d, partner, np_send.at[ch, y, dz]).wait_recv()
        for q in range(0, per, 2):
            p = ch * per + q
            rhs = jnp.concatenate([gn[p], gn[p + 1]], axis=1)
            res = mm(weights, rhs).astype(BF)
            for k in range(2):
                at = pl.ds(pl.multiple_of((p + k) * loc, loc), loc)
                for h in range(heads):
                    a2_sc[at, h * lanes:(h + 1) * lanes] = (
                        res[h * loc:(h + 1) * loc, k * lanes:(k + 1) * lanes])
        size = per * loc
        at = pl.ds(pl.multiple_of(ch * size, size), size)
        total = jnp.zeros((size, lanes), F32)
        rows = heads * lanes // 2
        for g in range(2):
            mean = mm(a2_sc[at, g * rows:(g + 1) * rows], bd_sc[g])
            gated = (gate_sc[at, g * wide:(g + 1) * wide] * mean).astype(BF)
            total += mm(gated, fin_sc[g * wide:(g + 1) * wide, :])
        for k in range(2):
            where = pl.ds(ch * per + k * half, per)
            piece = total[:, k * feat:(k + 1) * feat].reshape(per, loc, feat)
            out_ref[where] = (x_ref[where].astype(F32) + piece).astype(BF)
        return carry

    lax.fori_loop(0, chunks, average_chunk, 0)

    for dz in range(nz):
        if dz:
            r_copy(me, yside, rz_send.at[dz]).wait_send()
        r_copy(me, yside, ry_send.at[dz]).wait_send()
        for y in range(2):
            r_copy(me, yside, rp_send.at[y, dz]).wait_send()

    def drain(ch, carry):
        for dz in range(nz):
            if dz:
                n_copy(ch, me, yside, nz_send.at[ch, dz]).wait_send()
            n_copy(ch, me, yside, ny_send.at[ch, dz]).wait_send()
            for y in range(2):
                n_copy(ch, me, yside, np_send.at[ch, y, dz]).wait_send()
        return carry

    lax.fori_loop(0, chunks, drain, 0)
    save.wait()


def shards(row_count, x, pair, mask, tok, scale, former, latter, outw, gain, logitw, content, switch, final):
    seqs, loc, feat = x.shape
    span, zdim = pair.shape[1:]
    factor = former.shape[1]
    heads = logitw.shape[1]
    width = content.shape[1] // heads
    nz = row_count // 4
    chunks = 4
    half = seqs // 2
    lanes = 2 * feat
    pairs = loc // 2
    tiles = factor * seqs // 128
    vm = pl.BlockSpec(memory_space=pltpu.VMEM)
    hbm = pl.BlockSpec(memory_space=pl.ANY)
    dma = pltpu.SemaphoreType.DMA
    return pl.pallas_call(
        functools.partial(kernel, (nz, chunks)),
        out_shape=(jax.ShapeDtypeStruct(x.shape, x.dtype), jax.ShapeDtypeStruct(pair.shape, pair.dtype)),
        in_specs=[vm, hbm] + [vm] * 11,
        out_specs=(vm, hbm),
        scratch_shapes=[
            pltpu.VMEM((tiles + 1, span, 128), BF),
            pltpu.VMEM((half, span, lanes), BF),
            pltpu.VMEM((pairs, factor * seqs, 2 * zdim), BF),
            pltpu.VMEM((half * loc, lanes), F32),
            pltpu.VMEM((pairs, 2 * seqs, 128), BF),
            pltpu.VMEM((pairs * factor, 128), F32),
            pltpu.VMEM((factor * factor, zdim), F32),
            pltpu.VMEM((factor, factor * zdim), BF),
            pltpu.VMEM((pairs, 128, 2 * zdim), BF),
            pltpu.VMEM((4 * heads, 4 * zdim), BF),
            pltpu.VMEM((span // 128, heads * loc, 128), F32),
            pltpu.VMEM((2, heads * lanes // 2, heads * width), BF),
            pltpu.VMEM((2 * heads * width, lanes), BF),
            pltpu.VMEM((half * loc, 2 * heads * width), F32),
            pltpu.VMEM((half * loc, heads * lanes), BF),
            pltpu.VMEM((loc, span, zdim), BF),
            pltpu.VMEM((loc, span, zdim), BF),
            dma((row_count,)),
            dma((nz,)),
            dma((nz,)),
            dma((2, nz)),
            dma((chunks, row_count)),
            dma((chunks, nz)),
            dma((chunks, nz)),
            dma((chunks, 2, nz)),
            dma,
            dma,
        ],
        compiler_params=pltpu.CompilerParams(
            collective_id=0, has_side_effects=True, vmem_limit_bytes=60 * 1024 * 1024),
        name="msa_step",
    )(x, pair, mask, tok.reshape(1, span), scale.reshape(1, feat), former, latter, outw,
      gain.reshape(1, zdim), logitw, content, switch, final)


def solution(mesh):
    placed = (
        P("groups", "row", None),
        P(("groups", "row"), None, None),
        P("groups", "row"),
        P("groups"),
    ) + (P(),) * 9
    return jax.shard_map(
        functools.partial(shards, mesh.shape["row"]),
        mesh=mesh,
        in_specs=placed,
        out_specs=(P("groups", "row", None), P(("groups", "row"), None, None)),
        check_vma=False,
    )
```

```python
import functools

import jax
import jax.numpy as jnp
from jax import lax
from jax.experimental import pallas as pl
from jax.experimental.pallas import tpu as pltpu
from jax.sharding import PartitionSpec as P

F32 = jnp.float32
BF = jnp.bfloat16
MESH = pl.DeviceIdType.MESH
NT = (((1,), (1,)), ((), ()))


def mm(a, b):
    return jnp.dot(a, b, preferred_element_type=F32)


def iota(shape, dim):
    return lax.broadcasted_iota(jnp.int32, shape, dim)


def kernel(
    dims,
    *refs,
):
    count = 13
    sources, held = refs[:count], refs[count + 2:2 * count + 2]
    (x_ref, pair_in, mask_ref, tok_ref, scale_ref, former_ref, latter_ref, outw_ref,
     gain_ref, logitw_ref, content_ref, switch_ref, final_ref) = held
    out_ref, pair_new = refs[count:count + 2]
    (gr, gn, fold, n2_sc, lhs_sc, rt_sc, wf_sc, wl_sc, mr_sc, gw_sc, lg_sc, bd_sc, fin_sc,
    gate_sc, a2_sc,
    r_recv, rz_send, ry_send, rp_send, n_recv, nz_send, ny_send, np_send, in_sem) = refs[2 * count + 2:]
    loads = [pltpu.make_async_copy(a, b, in_sem.at[k]) for k, (a, b) in enumerate(zip(sources, held))]
    order = (0, 4, 2, 5, 6, 7, 9, 8, 10, 11, 12, 3, 1)
    for k in order:
        loads[k].start()
    nz, chunks = dims
    seqs, loc, feat = x_ref.shape
    half = seqs // 2
    lanes = 2 * feat
    pairs = loc // 2
    factor = former_ref.shape[0]
    zdim = outw_ref.shape[1]
    heads = logitw_ref.shape[0]
    width = content_ref.shape[1] // heads
    span = gn.shape[1] * loc
    tiles = factor * seqs // 128
    per = half // chunks
    half_rows = half * loc

    group = lax.axis_index("groups")
    me = lax.axis_index("row")
    core = lax.rem(me, 2)
    yy = lax.rem(me // 2, 2)
    zz = me // 4

    def dev(z, y, c):
        return (z * 2 + y) * 2 + c

    def far(dz):
        return lax.rem(zz + dz, nz)

    partner = dev(zz, yy, 1 - core)
    yside = dev(zz, 1 - yy, core)

    barrier = pltpu.get_barrier_semaphore()
    peers = [dev(far(dz), yy, core) for dz in range(1, nz)] + [yside, partner]
    for peer in peers:
        pl.semaphore_signal(barrier, inc=1, device_id=(group, peer), device_id_type=MESH)


    def r_copy(d, target, sem):
        view = gr.at[d]
        return pltpu.make_async_remote_copy(
            src_ref=view, dst_ref=view, send_sem=sem, recv_sem=r_recv.at[d],
            device_id=(group, target), device_id_type=MESH)

    def n_copy(ch, d, target, sem):
        view = gn.at[ch, d]
        return pltpu.make_async_remote_copy(
            src_ref=view, dst_ref=view, send_sem=sem, recv_sem=n_recv.at[ch, d],
            device_id=(group, target), device_id_type=MESH)

    for k in order[:5]:
        loads[k].wait()
    x = x_ref[...].astype(F32)
    center = jnp.mean(x, axis=-1, keepdims=True)
    spread = jnp.mean((x - center) ** 2, axis=-1, keepdims=True)
    normed = ((x - center) * lax.rsqrt(spread + 1e-05) * scale_ref[...][None]).astype(BF).astype(F32)
    n2 = jnp.concatenate(
        [normed[:half].reshape(half_rows, feat), normed[half:].reshape(half_rows, feat)], axis=1)
    n2_sc[...] = n2
    gn[:, me] = n2.astype(BF).reshape(chunks, per, loc, lanes)

    mask_pad = jnp.concatenate(
        [mask_ref[...].astype(F32), jnp.zeros((loc, 128 - seqs), F32)], axis=1)
    gr[me, tiles] = mask_pad.astype(BF)
    mask_sq = jnp.concatenate([mask_pad, jnp.zeros((128 - loc, 128), F32)], axis=0).T
    mask = mask_sq[:seqs]
    proj = jnp.concatenate(
        [former_ref[...].astype(F32), latter_ref[...].astype(F32),
         jnp.zeros((128 - 2 * factor, feat), F32)], axis=0).astype(BF)

    def rows_for(i):
        packed = n2_sc[pl.ds(i, half, stride=loc), :]
        rows = jnp.concatenate([packed[:, :feat], packed[:, feat:]], axis=0)
        return rows * mask[:, i:i + 1]

    for i2 in range(pairs):
        rows = jnp.concatenate([rows_for(i2), rows_for(i2 + pairs)], axis=0).astype(BF)
        both = lax.dot_general(rows, proj, NT, preferred_element_type=F32)
        lhs_sc[i2] = both.astype(BF)
        flipped = both.T
        rt_sc[pl.ds(i2 * factor, factor), :] = flipped[factor:2 * factor]
    low = iota((pairs, 128), 1) < seqs
    for t in range(tiles):
        a = rt_sc[pl.ds(2 * t, pairs, stride=factor), :]
        b = rt_sc[pl.ds(2 * t + 1, pairs, stride=factor), :]
        top = jnp.where(low, a, pltpu.roll(b, seqs, 1))
        bottom = jnp.where(low, pltpu.roll(a, seqs, 1), b)
        gr[me, t] = jnp.concatenate([top, bottom], axis=0).astype(BF)

    pl.semaphore_wait(barrier, nz + 1)
    r_copy(me, yside, ry_send.at[0]).start()
    for dz in range(1, nz):
        r_copy(me, dev(far(dz), yy, core), rz_send.at[dz]).start()
    r_copy(me, partner, rp_send.at[0, 0]).start()
    n_copy(0, me, yside, ny_send.at[0, 0]).start()
    for ch in range(chunks):
        for dz in range(1, nz):
            n_copy(ch, me, dev(far(dz), yy, core), nz_send.at[ch, dz]).start()

    for k in order[5:11]:
        loads[k].wait()
    wf_sc[...] = outw_ref[...].astype(F32)
    for e in range(factor):
        wl_sc[:, e * zdim:(e + 1) * zdim] = wf_sc[pl.ds(e, factor, stride=factor), :].astype(BF)

    def r_relay(dz):
        d = dev(far(dz), yy, core)
        r_copy(d, partner, ry_send.at[dz]).wait_recv()
        r_copy(d, yside, ry_send.at[dz]).start()
        r_copy(d, partner, rp_send.at[0, dz]).start()

    def fold_step(i2, carry):
        left = lhs_sc[i2][:, :factor]
        step = 8
        for e0 in range(0, factor, step):
            res = mm(left, wl_sc[:, e0 * zdim:(e0 + step) * zdim]).astype(BF)
            for e in range(e0, e0 + step):
                part = res[:, (e - e0) * zdim:(e - e0 + 1) * zdim]
                fold[i2, e * seqs:(e + 1) * seqs, :zdim] = part[:seqs]
                fold[i2, e * seqs:(e + 1) * seqs, zdim:] = part[seqs:]
        return carry

    lax.fori_loop(0, pairs // 2, fold_step, 0)
    r_relay(1)
    lax.fori_loop(pairs // 2, pairs, fold_step, 0)
    r_relay(nz - 1)

    for i2 in range(pairs):
        for k in range(2):
            col = mask_sq[:, i2 + k * pairs:i2 + k * pairs + 1]
            mr_sc[i2, :, k * zdim:(k + 1) * zdim] = jnp.broadcast_to(col, (128, zdim)).astype(BF)
    gw = logitw_ref[...] * gain_ref[...]
    g0 = gw.astype(BF).astype(F32)
    g1 = (gw - g0).astype(BF).astype(F32)
    g2 = gw - g0 - g1
    flat = jnp.concatenate([g0, g1, g2, jnp.zeros((heads, zdim), F32)], axis=0)
    ones = jnp.concatenate([jnp.zeros((3 * heads, zdim), F32), jnp.ones((heads, zdim), F32)], axis=0)
    gw_sc[...] = jnp.concatenate([flat, flat, ones, ones], axis=1).astype(BF)

    cols = heads * 2 * width
    pick = (iota((heads * width, cols), 0)
            == (iota((heads * width, cols), 1) // (2 * width)) * width
            + iota((heads * width, cols), 1) % width).astype(F32).astype(BF)
    content = mm(content_ref[...], pick)
    wide = cols // 2
    for g in range(2):
        part = jnp.concatenate([content[:, g * wide:(g + 1) * wide]] * heads, axis=0)
        keep = iota(part.shape, 0) // feat == iota(part.shape, 1) // width
        bd_sc[g] = jnp.where(keep, part, 0.0).astype(BF)
    switch = mm(switch_ref[...], pick)
    switch = jnp.concatenate([switch, switch], axis=0)
    keep = iota(switch.shape, 0) // feat == (iota(switch.shape, 1) // width) % 2
    switch = jnp.where(keep, switch, 0.0).astype(BF)
    fin = mm(final_ref[...], pick)
    fin = jnp.concatenate([fin, fin], axis=0)
    keep = iota(fin.shape, 0) // feat == (iota(fin.shape, 1) // width) % 2
    fin_sc[...] = jnp.where(keep, fin, 0.0).astype(BF)

    for dz in range(2, nz - 1):
        r_relay(dz)
    for ch in range(1, chunks):
        n_copy(ch, me, yside, ny_send.at[ch, 0]).start()
    for q in range(4):
        size = half_rows // 4
        pre = mm(n2_sc[q * size:(q + 1) * size, :].astype(BF), switch)
        gate_sc[q * size:(q + 1) * size, :] = jax.nn.sigmoid(pre)

    for dz in [0, 1] + list(range(nz - 1, 1, -1)):
        d = dev(far(dz), 1 - yy, core)
        r_copy(d, partner, rp_send.at[1, dz]).wait_recv()
        r_copy(d, partner, rp_send.at[1, dz]).start()
    for ch in range(chunks):
        n_copy(ch, me, partner, np_send.at[ch, 0, 0]).start()
    for y in range(2):
        for dz in range(nz):
            d = dev(far(dz), lax.rem(yy + y, 2), 1 - core)
            r_copy(d, partner, rp_send.at[y, dz]).wait_recv()
    for k in order[-2:]:
        loads[k].wait()

    real = tok_ref[...] == 1
    mean_of = jnp.full((zdim, zdim), 1.0 / zdim, F32).astype(BF)
    rel = pairs // chunks

    def n_relay(ch):
        for dz in range(1, nz):
            d = dev(far(dz), yy, core)
            n_copy(ch, d, yside, ny_send.at[ch, dz]).wait_recv()
            n_copy(ch, d, yside, ny_send.at[ch, dz]).start()
            n_copy(ch, d, partner, np_send.at[ch, 0, dz]).start()

    n_relay(0)

    def pair_step(i2, carry):
        lhs = jnp.concatenate([gr[:, t].reshape(span, 128) for t in range(tiles)], axis=1)
        acc = mm(lhs, fold[i2])
        counts = mm(gr[:, tiles].reshape(span, 128), mr_sc[i2])
        acc = acc / (1.0 + counts)
        for k in range(2):
            i = i2 + k * pairs
            new = (pair_in[i].astype(F32) + acc[:, k * zdim:(k + 1) * zdim]).astype(BF)
            pair_new[i] = new
            cent = new.astype(F32) - mm(new, mean_of)
            hi = cent.astype(BF)
            lo = (cent - hi.astype(F32)).astype(BF)
            sq = cent * cent
            sh = sq.astype(BF)
            sl = (sq - sh.astype(F32)).astype(BF)
            rhs = jnp.concatenate([hi, lo, sh, sl], axis=1)
            res = lax.dot_general(gw_sc[...], rhs, NT, preferred_element_type=F32)
            total = res[:heads] + res[heads:2 * heads] + res[2 * heads:3 * heads]
            logits = total * lax.rsqrt(res[3 * heads:] / zdim + 1e-05)
            logits = jnp.where(real, logits, -1000000000.0)
            for t in range(span // 128):
                lg_sc[t, pl.ds(i, heads, stride=loc), :] = logits[:, t * 128:(t + 1) * 128]
        ch = i2 // rel

        @pl.when((lax.rem(i2, rel) == 0) & (ch + 1 < chunks))
        def _():
            n_relay(ch + 1)

        @pl.when(lax.rem(i2, rel) == rel - 1)
        def _():
            for dz in range(nz):
                d = dev(far(dz), 1 - yy, core)
                n_copy(ch, d, partner, np_send.at[ch, 1, dz]).wait_recv()
                n_copy(ch, d, partner, np_send.at[ch, 1, dz]).start()

        return carry

    lax.fori_loop(0, pairs, pair_step, 0)

    logits = jnp.concatenate([lg_sc[t] for t in range(span // 128)], axis=1)
    top = jnp.max(logits, axis=1, keepdims=True)
    raised = jnp.exp(logits - top)
    weights = (raised / jnp.sum(raised, axis=1, keepdims=True)).astype(BF)

    def average_chunk(ch, carry):
        for y in range(2):
            for dz in range(nz):
                d = dev(far(dz), lax.rem(yy + y, 2), 1 - core)
                n_copy(ch, d, partner, np_send.at[ch, y, dz]).wait_recv()
        for q in range(0, per, 2):
            p = ch * per + q
            rhs = jnp.concatenate([gn[ch, :, q + k].reshape(span, lanes) for k in range(2)], axis=1)
            res = mm(weights, rhs).astype(BF)
            for k in range(2):
                at = pl.ds(pl.multiple_of((p + k) * loc, loc), loc)
                for h in range(heads):
                    a2_sc[at, h * lanes:(h + 1) * lanes] = (
                        res[h * loc:(h + 1) * loc, k * lanes:(k + 1) * lanes])
        size = per * loc
        at = pl.ds(pl.multiple_of(ch * size, size), size)
        total = jnp.zeros((size, lanes), F32)
        rows = heads * lanes // 2
        for g in range(2):
            mean = mm(a2_sc[at, g * rows:(g + 1) * rows], bd_sc[g])
            gated = (gate_sc[at, g * wide:(g + 1) * wide] * mean).astype(BF)
            total += lax.dot_general(
                gated, fin_sc[:, g * wide:(g + 1) * wide], NT, preferred_element_type=F32)
        for k in range(2):
            where = pl.ds(ch * per + k * half, per)
            piece = total[:, k * feat:(k + 1) * feat].reshape(per, loc, feat)
            out_ref[where] = (x_ref[where].astype(F32) + piece).astype(BF)
        return carry

    lax.fori_loop(0, chunks, average_chunk, 0)

    for dz in range(nz):
        if dz:
            r_copy(me, yside, rz_send.at[dz]).wait_send()
        r_copy(me, yside, ry_send.at[dz]).wait_send()
        for y in range(2):
            r_copy(me, yside, rp_send.at[y, dz]).wait_send()

    def drain(ch, carry):
        for dz in range(nz):
            if dz:
                n_copy(ch, me, yside, nz_send.at[ch, dz]).wait_send()
            n_copy(ch, me, yside, ny_send.at[ch, dz]).wait_send()
            for y in range(2):
                n_copy(ch, me, yside, np_send.at[ch, y, dz]).wait_send()
        return carry

    lax.fori_loop(0, chunks, drain, 0)


def shards(row_count, x, pair, mask, tok, scale, former, latter, outw, gain, logitw, content, switch, final):
    seqs, loc, feat = x.shape
    span, zdim = pair.shape[1:]
    factor = former.shape[1]
    heads = logitw.shape[1]
    width = content.shape[1] // heads
    nz = row_count // 4
    chunks = 4
    half = seqs // 2
    lanes = 2 * feat
    pairs = loc // 2
    tiles = factor * seqs // 128
    vm = pl.BlockSpec(memory_space=pltpu.VMEM)
    hbm = pl.BlockSpec(memory_space=pltpu.MemorySpace.HBM)
    dma = pltpu.SemaphoreType.DMA
    operands = (
        x, pair, mask.T, tok.reshape(1, span), scale.reshape(1, feat), former.T, latter.T, outw,
        gain.reshape(1, zdim), logitw.T, content, switch, final.T)
    operands = tuple(pltpu.with_memory_space_constraint(a, pltpu.MemorySpace.HBM) for a in operands)
    return pl.pallas_call(
        functools.partial(kernel, (nz, chunks)),
        out_shape=(jax.ShapeDtypeStruct(x.shape, x.dtype), jax.ShapeDtypeStruct(pair.shape, pair.dtype)),
        in_specs=[hbm] * 13,
        out_specs=(vm, vm),
        scratch_shapes=[pltpu.VMEM(a.shape, a.dtype) for a in operands] + [
            pltpu.VMEM((row_count, tiles + 1, loc, 128), BF),
            pltpu.VMEM((chunks, row_count, half // chunks, loc, lanes), BF),
            pltpu.VMEM((pairs, factor * seqs, 2 * zdim), BF),
            pltpu.VMEM((half * loc, lanes), F32),
            pltpu.VMEM((pairs, 2 * seqs, 128), BF),
            pltpu.VMEM((pairs * factor, 128), F32),
            pltpu.VMEM((factor * factor, zdim), F32),
            pltpu.VMEM((factor, factor * zdim), BF),
            pltpu.VMEM((pairs, 128, 2 * zdim), BF),
            pltpu.VMEM((4 * heads, 4 * zdim), BF),
            pltpu.VMEM((span // 128, heads * loc, 128), F32),
            pltpu.VMEM((2, heads * lanes // 2, heads * width), BF),
            pltpu.VMEM((lanes, 2 * heads * width), BF),
            pltpu.VMEM((half * loc, 2 * heads * width), F32),
            pltpu.VMEM((half * loc, heads * lanes), BF),
            dma((row_count,)),
            dma((nz,)),
            dma((nz,)),
            dma((2, nz)),
            dma((chunks, row_count)),
            dma((chunks, nz)),
            dma((chunks, nz)),
            dma((chunks, 2, nz)),
            dma((13,)),
        ],
        compiler_params=pltpu.CompilerParams(
            collective_id=0, has_side_effects=True, vmem_limit_bytes=32 * 1024 * 1024),
        name="msa_step",
    )(*operands)


def solution(mesh):
    placed = (
        P("groups", "row", None),
        P(("groups", "row"), None, None),
        P("groups", "row"),
        P("groups"),
    ) + (P(),) * 9
    return jax.shard_map(
        functools.partial(shards, mesh.shape["row"]),
        mesh=mesh,
        in_specs=placed,
        out_specs=(P("groups", "row", None), P(("groups", "row"), None, None)),
        check_vma=False,
    )
```

```python
import functools

import jax
import jax.numpy as jnp
from jax import lax
from jax.experimental import pallas as pl
from jax.experimental.pallas import tpu as pltpu
from jax.sharding import PartitionSpec as P

F32 = jnp.float32
BF = jnp.bfloat16
MESH = pl.DeviceIdType.MESH
NT = (((1,), (1,)), ((), ()))


def mm(a, b):
    return jnp.dot(a, b, preferred_element_type=F32)


def iota(shape, dim):
    return lax.broadcasted_iota(jnp.int32, shape, dim)


def kernel(
    dims,
    *refs,
):
    count = 13
    sources, held = refs[:count], refs[count + 2:2 * count + 2]
    (x_ref, pair_in, mask_ref, tok_ref, scale_ref, former_ref, latter_ref, outw_ref,
     gain_ref, logitw_ref, content_ref, switch_ref, final_ref) = held
    out_ref, pair_new = refs[count:count + 2]
    (gr, gn, fold, n2_sc, lhs_sc, rt_sc, wf_sc, wl_sc, mr_sc, gw_sc, lg_sc, bd_sc, fin_sc,
    gate_sc, a2_sc,
    r_recv, rz_send, ry_send, rp_send, n_recv, nz_send, ny_send, np_send, in_sem) = refs[2 * count + 2:]
    loads = [pltpu.make_async_copy(a, b, in_sem.at[k]) for k, (a, b) in enumerate(zip(sources, held))]
    order = (0, 4, 2, 5, 6, 7, 9, 8, 10, 11, 12, 3, 1)
    for k in order:
        loads[k].start()
    nz, chunks = dims
    seqs, loc, feat = x_ref.shape
    half = seqs // 2
    lanes = 2 * feat
    pairs = loc // 2
    factor = former_ref.shape[0]
    zdim = outw_ref.shape[1]
    heads = logitw_ref.shape[0]
    width = content_ref.shape[1] // heads
    span = gn.shape[1] * loc
    tiles = factor * seqs // 128
    per = half // chunks
    half_rows = half * loc

    group = lax.axis_index("groups")
    me = lax.axis_index("row")
    core = lax.rem(me, 2)
    yy = lax.rem(me // 2, 2)
    zz = me // 4

    def dev(z, y, c):
        return (z * 2 + y) * 2 + c

    def far(dz):
        return lax.rem(zz + dz, nz)

    partner = dev(zz, yy, 1 - core)
    yside = dev(zz, 1 - yy, core)

    barrier = pltpu.get_barrier_semaphore()
    peers = [dev(far(dz), yy, core) for dz in range(1, nz)] + [yside, partner]
    for peer in peers:
        pl.semaphore_signal(barrier, inc=1, device_id=(group, peer), device_id_type=MESH)


    def r_copy(d, target, sem):
        view = gr.at[d]
        return pltpu.make_async_remote_copy(
            src_ref=view, dst_ref=view, send_sem=sem, recv_sem=r_recv.at[d],
            device_id=(group, target), device_id_type=MESH)

    def n_copy(ch, d, target, sem):
        view = gn.at[ch, d]
        return pltpu.make_async_remote_copy(
            src_ref=view, dst_ref=view, send_sem=sem, recv_sem=n_recv.at[ch, d],
            device_id=(group, target), device_id_type=MESH)

    for k in order[:5]:
        loads[k].wait()
    x = x_ref[...].astype(F32)
    center = jnp.mean(x, axis=-1, keepdims=True)
    spread = jnp.mean((x - center) ** 2, axis=-1, keepdims=True)
    normed = ((x - center) * lax.rsqrt(spread + 1e-05) * scale_ref[...][None]).astype(BF).astype(F32)
    n2 = jnp.concatenate(
        [normed[:half].reshape(half_rows, feat), normed[half:].reshape(half_rows, feat)], axis=1)
    n2_sc[...] = n2
    gn[:, me] = n2.astype(BF).reshape(chunks, per, loc, lanes)

    mask_pad = jnp.concatenate(
        [mask_ref[...].astype(F32), jnp.zeros((loc, 128 - seqs), F32)], axis=1)
    gr[me, tiles] = mask_pad.astype(BF)
    mask_sq = jnp.concatenate([mask_pad, jnp.zeros((128 - loc, 128), F32)], axis=0).T
    mask = mask_sq[:seqs]
    proj = jnp.concatenate(
        [former_ref[...].astype(F32), latter_ref[...].astype(F32),
         jnp.zeros((128 - 2 * factor, feat), F32)], axis=0).astype(BF)

    def rows_for(i):
        packed = n2_sc[pl.ds(i, half, stride=loc), :]
        rows = jnp.concatenate([packed[:, :feat], packed[:, feat:]], axis=0)
        return rows * mask[:, i:i + 1]

    for i2 in range(pairs):
        rows = jnp.concatenate([rows_for(i2), rows_for(i2 + pairs)], axis=0).astype(BF)
        both = lax.dot_general(rows, proj, NT, preferred_element_type=F32)
        lhs_sc[i2] = both.astype(BF)
        flipped = both.T
        rt_sc[pl.ds(i2 * factor, factor), :] = flipped[factor:2 * factor]
    low = iota((pairs, 128), 1) < seqs
    for t in range(tiles):
        a = rt_sc[pl.ds(2 * t, pairs, stride=factor), :]
        b = rt_sc[pl.ds(2 * t + 1, pairs, stride=factor), :]
        top = jnp.where(low, a, pltpu.roll(b, seqs, 1))
        bottom = jnp.where(low, pltpu.roll(a, seqs, 1), b)
        gr[me, t] = jnp.concatenate([top, bottom], axis=0).astype(BF)

    pl.semaphore_wait(barrier, nz + 1)
    r_copy(me, yside, ry_send.at[0]).start()
    for dz in range(1, nz):
        r_copy(me, dev(far(dz), yy, core), rz_send.at[dz]).start()
    r_copy(me, partner, rp_send.at[0, 0]).start()
    n_copy(0, me, yside, ny_send.at[0, 0]).start()
    for ch in range(chunks):
        for dz in range(1, nz):
            n_copy(ch, me, dev(far(dz), yy, core), nz_send.at[ch, dz]).start()

    for k in order[5:11]:
        loads[k].wait()
    wf_sc[...] = outw_ref[...].astype(F32)
    for e in range(factor):
        wl_sc[:, e * zdim:(e + 1) * zdim] = wf_sc[pl.ds(e, factor, stride=factor), :].astype(BF)

    def r_relay(dz):
        d = dev(far(dz), yy, core)
        r_copy(d, partner, ry_send.at[dz]).wait_recv()
        r_copy(d, yside, ry_send.at[dz]).start()
        r_copy(d, partner, rp_send.at[0, dz]).start()

    def fold_step(i2, carry):
        left = lhs_sc[i2][:, :factor]
        step = 8
        for e0 in range(0, factor, step):
            res = mm(left, wl_sc[:, e0 * zdim:(e0 + step) * zdim]).astype(BF)
            for e in range(e0, e0 + step):
                part = res[:, (e - e0) * zdim:(e - e0 + 1) * zdim]
                fold[i2, e * seqs:(e + 1) * seqs, :zdim] = part[:seqs]
                fold[i2, e * seqs:(e + 1) * seqs, zdim:] = part[seqs:]
        return carry

    lax.fori_loop(0, pairs // 2, fold_step, 0)
    r_relay(1)
    lax.fori_loop(pairs // 2, pairs, fold_step, 0)
    r_relay(nz - 1)

    for i2 in range(pairs):
        for k in range(2):
            col = mask_sq[:, i2 + k * pairs:i2 + k * pairs + 1]
            mr_sc[i2, :, k * zdim:(k + 1) * zdim] = jnp.broadcast_to(col, (128, zdim)).astype(BF)
    gw = logitw_ref[...] * gain_ref[...]
    g0 = gw.astype(BF).astype(F32)
    g1 = (gw - g0).astype(BF).astype(F32)
    g2 = gw - g0 - g1
    flat = jnp.concatenate([g0, g1, g2, jnp.zeros((heads, zdim), F32)], axis=0)
    ones = jnp.concatenate([jnp.zeros((3 * heads, zdim), F32), jnp.ones((heads, zdim), F32)], axis=0)
    gw_sc[...] = jnp.concatenate([flat, flat, ones, ones], axis=1).astype(BF)

    cols = heads * 2 * width
    pick = (iota((heads * width, cols), 0)
            == (iota((heads * width, cols), 1) // (2 * width)) * width
            + iota((heads * width, cols), 1) % width).astype(F32).astype(BF)
    content = mm(content_ref[...], pick)
    wide = cols // 2
    for g in range(2):
        part = jnp.concatenate([content[:, g * wide:(g + 1) * wide]] * heads, axis=0)
        keep = iota(part.shape, 0) // feat == iota(part.shape, 1) // width
        bd_sc[g] = jnp.where(keep, part, 0.0).astype(BF)
    switch = mm(switch_ref[...], pick)
    switch = jnp.concatenate([switch, switch], axis=0)
    keep = iota(switch.shape, 0) // feat == (iota(switch.shape, 1) // width) % 2
    switch = jnp.where(keep, switch, 0.0).astype(BF)
    fin = mm(final_ref[...], pick)
    fin = jnp.concatenate([fin, fin], axis=0)
    keep = iota(fin.shape, 0) // feat == (iota(fin.shape, 1) // width) % 2
    fin_sc[...] = jnp.where(keep, fin, 0.0).astype(BF)

    for dz in range(2, nz - 1):
        r_relay(dz)
    for ch in range(1, chunks):
        n_copy(ch, me, yside, ny_send.at[ch, 0]).start()
    for q in range(4):
        size = half_rows // 4
        pre = mm(n2_sc[q * size:(q + 1) * size, :].astype(BF), switch)
        gate_sc[q * size:(q + 1) * size, :] = jax.nn.sigmoid(pre)

    for dz in [0, 1] + list(range(nz - 1, 1, -1)):
        d = dev(far(dz), 1 - yy, core)
        r_copy(d, partner, rp_send.at[1, dz]).wait_recv()
        r_copy(d, partner, rp_send.at[1, dz]).start()
    for ch in range(chunks):
        n_copy(ch, me, partner, np_send.at[ch, 0, 0]).start()
    for y in range(2):
        for dz in range(nz):
            d = dev(far(dz), lax.rem(yy + y, 2), 1 - core)
            r_copy(d, partner, rp_send.at[y, dz]).wait_recv()
    for k in order[-2:]:
        loads[k].wait()

    real = tok_ref[...] == 1
    mean_of = jnp.full((zdim, zdim), 1.0 / zdim, F32).astype(BF)
    rel = pairs // chunks

    def n_relay(ch):
        for dz in range(1, nz):
            d = dev(far(dz), yy, core)
            n_copy(ch, d, yside, ny_send.at[ch, dz]).wait_recv()
            n_copy(ch, d, yside, ny_send.at[ch, dz]).start()
            n_copy(ch, d, partner, np_send.at[ch, 0, dz]).start()

    n_relay(0)

    def pair_step(i2, carry):
        lhs = jnp.concatenate([gr[:, t].reshape(span, 128) for t in range(tiles)], axis=1)
        acc = mm(lhs, fold[i2])
        counts = mm(gr[:, tiles].reshape(span, 128), mr_sc[i2])
        acc = acc / (1.0 + counts)
        for k in range(2):
            i = i2 + k * pairs
            new = (pair_in[i].astype(F32) + acc[:, k * zdim:(k + 1) * zdim]).astype(BF)
            pair_new[i] = new
            cent = new.astype(F32) - mm(new, mean_of)
            hi = cent.astype(BF)
            lo = (cent - hi.astype(F32)).astype(BF)
            sq = cent * cent
            sh = sq.astype(BF)
            sl = (sq - sh.astype(F32)).astype(BF)
            rhs = jnp.concatenate([hi, lo, sh, sl], axis=1)
            res = lax.dot_general(gw_sc[...], rhs, NT, preferred_element_type=F32)
            total = res[:heads] + res[heads:2 * heads] + res[2 * heads:3 * heads]
            logits = total * lax.rsqrt(res[3 * heads:] / zdim + 1e-05)
            logits = jnp.where(real, logits, -1000000000.0)
            for t in range(span // 128):
                lg_sc[t, pl.ds(i, heads, stride=loc), :] = logits[:, t * 128:(t + 1) * 128]
        ch = i2 // rel

        @pl.when((lax.rem(i2, rel) == 0) & (ch + 1 < chunks))
        def _():
            n_relay(ch + 1)

        @pl.when(lax.rem(i2, rel) == rel - 1)
        def _():
            for dz in range(nz):
                d = dev(far(dz), 1 - yy, core)
                n_copy(ch, d, partner, np_send.at[ch, 1, dz]).wait_recv()
                n_copy(ch, d, partner, np_send.at[ch, 1, dz]).start()

        return carry

    lax.fori_loop(0, pairs, pair_step, 0)

    logits = jnp.concatenate([lg_sc[t] for t in range(span // 128)], axis=1)
    top = jnp.max(logits, axis=1, keepdims=True)
    raised = jnp.exp(logits - top)
    weights = (raised / jnp.sum(raised, axis=1, keepdims=True)).astype(BF)

    def average_chunk(ch, carry):
        for y in range(2):
            for dz in range(nz):
                d = dev(far(dz), lax.rem(yy + y, 2), 1 - core)
                n_copy(ch, d, partner, np_send.at[ch, y, dz]).wait_recv()
        for q in range(0, per, 2):
            p = ch * per + q
            rhs = jnp.concatenate([gn[ch, :, q + k].reshape(span, lanes) for k in range(2)], axis=1)
            res = mm(weights, rhs).astype(BF)
            for k in range(2):
                at = pl.ds(pl.multiple_of((p + k) * loc, loc), loc)
                for h in range(heads):
                    a2_sc[at, h * lanes:(h + 1) * lanes] = (
                        res[h * loc:(h + 1) * loc, k * lanes:(k + 1) * lanes])
        size = per * loc
        at = pl.ds(pl.multiple_of(ch * size, size), size)
        total = jnp.zeros((size, lanes), F32)
        rows = heads * lanes // 2
        for g in range(2):
            mean = mm(a2_sc[at, g * rows:(g + 1) * rows], bd_sc[g])
            gated = (gate_sc[at, g * wide:(g + 1) * wide] * mean).astype(BF)
            total += lax.dot_general(
                gated, fin_sc[:, g * wide:(g + 1) * wide], NT, preferred_element_type=F32)
        for k in range(2):
            where = pl.ds(ch * per + k * half, per)
            piece = total[:, k * feat:(k + 1) * feat].reshape(per, loc, feat)
            out_ref[where] = (x_ref[where].astype(F32) + piece).astype(BF)
        return carry

    lax.fori_loop(0, chunks, average_chunk, 0)

    for dz in range(nz):
        if dz:
            r_copy(me, yside, rz_send.at[dz]).wait_send()
        r_copy(me, yside, ry_send.at[dz]).wait_send()
        for y in range(2):
            r_copy(me, yside, rp_send.at[y, dz]).wait_send()

    def drain(ch, carry):
        for dz in range(nz):
            if dz:
                n_copy(ch, me, yside, nz_send.at[ch, dz]).wait_send()
            n_copy(ch, me, yside, ny_send.at[ch, dz]).wait_send()
            for y in range(2):
                n_copy(ch, me, yside, np_send.at[ch, y, dz]).wait_send()
        return carry

    lax.fori_loop(0, chunks, drain, 0)


def shards(row_count, x, pair, mask, tok, scale, former, latter, outw, gain, logitw, content, switch, final):
    seqs, loc, feat = x.shape
    span, zdim = pair.shape[1:]
    factor = former.shape[1]
    heads = logitw.shape[1]
    width = content.shape[1] // heads
    nz = row_count // 4
    chunks = 2
    half = seqs // 2
    lanes = 2 * feat
    pairs = loc // 2
    tiles = factor * seqs // 128
    vm = pl.BlockSpec(memory_space=pltpu.VMEM)
    hbm = pl.BlockSpec(memory_space=pltpu.MemorySpace.HBM)
    dma = pltpu.SemaphoreType.DMA
    operands = (
        x, pair, mask.T, tok.reshape(1, span), scale.reshape(1, feat), former.T, latter.T, outw,
        gain.reshape(1, zdim), logitw.T, content, switch, final.T)
    operands = tuple(pltpu.with_memory_space_constraint(a, pltpu.MemorySpace.HBM) for a in operands)
    return pl.pallas_call(
        functools.partial(kernel, (nz, chunks)),
        out_shape=(jax.ShapeDtypeStruct(x.shape, x.dtype), jax.ShapeDtypeStruct(pair.shape, pair.dtype)),
        in_specs=[hbm] * 13,
        out_specs=(vm, vm),
        scratch_shapes=[pltpu.VMEM(a.shape, a.dtype) for a in operands] + [
            pltpu.VMEM((row_count, tiles + 1, loc, 128), BF),
            pltpu.VMEM((chunks, row_count, half // chunks, loc, lanes), BF),
            pltpu.VMEM((pairs, factor * seqs, 2 * zdim), BF),
            pltpu.VMEM((half * loc, lanes), F32),
            pltpu.VMEM((pairs, 2 * seqs, 128), BF),
            pltpu.VMEM((pairs * factor, 128), F32),
            pltpu.VMEM((factor * factor, zdim), F32),
            pltpu.VMEM((factor, factor * zdim), BF),
            pltpu.VMEM((pairs, 128, 2 * zdim), BF),
            pltpu.VMEM((4 * heads, 4 * zdim), BF),
            pltpu.VMEM((span // 128, heads * loc, 128), F32),
            pltpu.VMEM((2, heads * lanes // 2, heads * width), BF),
            pltpu.VMEM((lanes, 2 * heads * width), BF),
            pltpu.VMEM((half * loc, 2 * heads * width), F32),
            pltpu.VMEM((half * loc, heads * lanes), BF),
            dma((row_count,)),
            dma((nz,)),
            dma((nz,)),
            dma((2, nz)),
            dma((chunks, row_count)),
            dma((chunks, nz)),
            dma((chunks, nz)),
            dma((chunks, 2, nz)),
            dma((13,)),
        ],
        compiler_params=pltpu.CompilerParams(
            collective_id=0, has_side_effects=True, vmem_limit_bytes=32 * 1024 * 1024),
        name="msa_step",
    )(*operands)


def solution(mesh):
    placed = (
        P("groups", "row", None),
        P(("groups", "row"), None, None),
        P("groups", "row"),
        P("groups"),
    ) + (P(),) * 9
    return jax.shard_map(
        functools.partial(shards, mesh.shape["row"]),
        mesh=mesh,
        in_specs=placed,
        out_specs=(P("groups", "row", None), P(("groups", "row"), None, None)),
        check_vma=False,
    )
```
